32 devices in a mesh: dp: 4 (over x, core), section: 4 (over z), expert: 2 (over y).
Axes of the slice: x: 2, y: 2, z: 4, core: 2. Of those that a mesh axis runs over, the one named last changes fastest.
Arguments:
- tokens: bfloat16 [8192, 4096], P(('dp', 'section')), may hold values from -90 to 90
- w_query: bfloat16 [4096, 2048], P(None, 'expert'), may hold values from -0.09375 to 0.09375
- w_key: bfloat16 [4096, 1024], P(None, 'expert'), may hold values from -0.09375 to 0.09375
- w_value: bfloat16 [4096, 1024], P(None, 'expert'), may hold values from -0.09375 to 0.09375
- w_out: bfloat16 [2048, 4096], P('expert'), may hold values from -0.125 to 0.125
- w_gate: bfloat16 [2, 7168, 4096], P('expert', ('dp', 'section')), may hold values from -0.09375 to 0.09375
- w_up: bfloat16 [2, 7168, 4096], P('expert', ('dp', 'section')), may hold values from -0.09375 to 0.09375
- w_down: bfloat16 [2, 7168, 4096], P('expert', ('dp', 'section')), may hold values from -0.0625 to 0.0625
- route: int32 [128, 1], P(('dp', 'section')), may hold values from 0 to 1; in each aligned block of 8 rows (0 to 7, 8 to 15, ...) at most 5 rows name the same one
- old_out: bfloat16 [128, 64, 4096], P(('dp', 'section'), 'expert'), may hold values from -6 to 6
- cotangent: bfloat16 [8192, 4096], P(('dp', 'section')), may hold values from -6 to 6
Outputs:
- joined: bfloat16 [128, 64, 4096], P(('dp', 'section'), 'expert')
- divergence: float32 [128, 64], P(('dp', 'section'), 'expert')
- grad_out_t: float32 [4096, 2048], P(('dp', 'section'), 'expert')
The draws below stay inside these ranges and needn't reach their ends.
Inputs may be any that keep to these rules, and one draw needn't show every extreme that they name: `route`: blocks routed to experts 1 and above go to new experts. Among the 8 blocks of one replica no expert is named more than 5 times, and some replica names one expert exactly 5 times in every draw.
All inputs are finite; a program needn't handle non-finite values.
Results may differ from the reference program's by a relative error of at most 0.025.
Values may be sent and summed in bfloat16 or wider, within the bound.
A program may use at most 192 MiB of HBM per device.

```python
import math
import jax
import jax.numpy as jnp
import numpy as np
from jax import lax

D = 4096
HEADS = 16
KV_HEADS = 8
HEAD_DIM = 128
FFW = 7168
BLOCK = 64
SEQ = 512
EXPERTS = 2
OLD = 1
NB = 8
NBT = 128
TOKENS = 8192
CAP = 5
N_DP = 4
N_SECTION = 4


def draw_tokens(key, part):
    noise = jax.random.truncated_normal(jax.random.fold_in(key, 11), -6.0, 6.0, (TOKENS, D), jnp.float32)
    return noise.astype(jnp.bfloat16)


def strengthened(values, stream_key, source, target, blocks, factor):
    def block_of(axis_at):
        return (jnp.arange(values.shape[axis_at]) // (values.shape[axis_at] // blocks)).reshape((-1,) + (1,) * (values.ndim - 1 - axis_at))

    one_side = jax.random.permutation(stream_key, blocks)[block_of(target)]
    other_side = (block_of(target) + blocks // 2) % blocks
    return jnp.where((block_of(source) == one_side) | (block_of(source) == other_side), factor * values, values)


def levels(stream_key, shape, shards, low, largest):
    gain, own = 1.0, jax.random.fold_in(stream_key, 6)
    for position, shards_of in shards:
        heights = jnp.exp(jax.random.uniform(jax.random.fold_in(own, position), (shards_of,), jnp.float32, low / len(shards), largest / len(shards)))
        gain = gain * jnp.repeat(heights, shape[position] // shards_of).reshape([-1 if axis == position else 1 for axis in range(len(shape))])
    return gain


def deal_out(key, own, number, rows, count, top, reach, lean):
    order = jax.random.permutation(key, count)
    packed, ordinary = portions_of(count, rows * top, reach, lean, True), portions_of(count, rows * top, reach, lean, False)
    places = jnp.arange(count)

    def named(lengths, turn):
        used = int((lengths > 0).sum())
        fixed = max(1, used // 4)
        passed = fixed + (places - fixed + turn * (used - fixed)) % max(1, count - fixed)
        return jnp.zeros((count,), jnp.int32).at[order[jnp.where(places < fixed, places, passed)]].set(jnp.asarray(lengths, jnp.int32))

    lengths = jnp.where(number % 4 == 0, named(packed, number // 4), named(ordinary, number - number // 4 - 1))
    mixed = jax.random.permutation(jax.random.fold_in(own, 3), count)
    source_of, taker = mixed[0:count // 2 * 2:2], mixed[1:count // 2 * 2:2]
    margin = jnp.minimum(lengths[source_of] - 1, reach - lengths[taker]) // 2
    margin = jnp.where((source_of == order[0]) | (taker == order[0]) | (lengths[taker] == 0), 0, jnp.maximum(margin, 0))
    passed = jax.random.randint(jax.random.fold_in(own, 4), (count // 2,), 0, 1 << 20) % (margin + 1)
    lengths = lengths.at[source_of].add(-passed).at[taker].add(passed)
    items = jnp.searchsorted(jnp.cumsum(lengths), jnp.arange(rows * top), side="right").astype(jnp.int32)
    listing = items.reshape(top, rows).T
    listing = listing[jax.random.permutation(jax.random.fold_in(own, 1), rows)]
    turn = jax.random.randint(jax.random.fold_in(own, 2), (rows, 1), 0, top)
    return jnp.take_along_axis(listing, (jnp.arange(top)[None, :] + turn) % top, axis=1)


def portions_of(amount, total, reach, lean, full):
    weights = [(1 << 20) // math.isqrt(grade ** lean) + 1 for grade in range(1, amount + 1)]
    largest = reach if full else min(reach, max(-(-total // amount), total * weights[0] // sum(weights)))
    least = 1 if total - largest >= amount - 1 else 0
    given, rest = [largest] + [least] * (amount - 1), total - largest - least * (amount - 1)
    while rest > 0:
        movable = [i for i in range(1, amount) if given[i] < largest] or [i for i in range(1, amount) if given[i] < reach]
        whole, left = sum([weights[i] for i in movable]), rest
        for i in movable:
            extra = min(reach - given[i], max(1, left * weights[i] // whole), rest)
            given[i] = given[i] + extra
            rest = rest - extra
    return np.array(given)


def gaussian(own_key, shape, deviation, limit, cuts=(), held_as=jnp.bfloat16):
    array = deviation * jax.random.normal(own_key, shape, jnp.float32)
    if cuts:
        array = array * levels(own_key, shape, cuts, -0.22, 0.18)
    return jnp.clip(array, -limit, limit).astype(held_as)


def bell_draw_with(key, extent, spread, reach, split, heavy, dtype=jnp.bfloat16):
    entries = spread * jax.random.normal(key, extent, jnp.float32)
    if split:
        entries = entries * levels(key, extent, split, -0.22, 0.18)
    return jnp.clip(strengthened(entries, jax.random.fold_in(key, 3), *heavy), -reach, reach).astype(dtype)


def setup_inputs(seed: int = 0) -> dict:
    splits = jax.random.split(jax.random.key(seed), 12)
    tokens = draw_tokens(jax.random.fold_in(splits[11], 71), 0)
    w_query = gaussian(splits[1], (D, HEADS * HEAD_DIM), D ** -0.5, 0.09375, ((1, 2),))
    w_key = gaussian(splits[2], (D, KV_HEADS * HEAD_DIM), D ** -0.5, 0.09375, ((1, 2),))
    w_value = gaussian(splits[3], (D, KV_HEADS * HEAD_DIM), D ** -0.5, 0.09375, ((1, 2),))
    w_out = gaussian(splits[4], (HEADS * HEAD_DIM, D), (HEADS * HEAD_DIM) ** -0.5, 0.125, ((0, 2),))
    w_gate = gaussian(splits[5], (EXPERTS, FFW, D), D ** -0.5, 0.09375, ((0, 2), (1, 16)))
    w_up = gaussian(splits[6], (EXPERTS, FFW, D), D ** -0.5, 0.09375, ((0, 2), (1, 16)))
    w_down = gaussian(splits[7], (EXPERTS, FFW, D), FFW ** -0.5, 0.0625, ((0, 2), (1, 16)))
    route_keys = jax.random.split(jax.random.fold_in(splits[8], 1), NBT // NB)
    route_turns = jax.random.permutation(jax.random.fold_in(splits[8], 3), NBT // NB)
    route = jax.vmap(lambda own, number: deal_out(jax.random.fold_in(splits[8], 2), own, number, NB, EXPERTS, 1, CAP, 2))(route_keys, route_turns).reshape((NBT, 1))
    old_out = gaussian(splits[9], (NBT, BLOCK, D), 1.0, 6.0, ((0, 16), (1, 2)))
    cotangent = bell_draw_with(splits[10], (TOKENS, D), 1.0, 6.0, ((0, 16),), (0, 1, 16, 2.0))
    return {"tokens": tokens, "w_query": w_query, "w_key": w_key, "w_value": w_value, "w_out": w_out, "w_gate": w_gate, "w_up": w_up, "w_down": w_down, "route": route, "old_out": old_out, "cotangent": cotangent}


def attend_all(sequence, w_query, w_key, w_value):
    length = sequence.shape[0]
    group = HEADS // KV_HEADS
    queries = jnp.dot(sequence, w_query, preferred_element_type=jnp.float32).astype(jnp.bfloat16)
    keys = jnp.dot(sequence, w_key, preferred_element_type=jnp.float32).astype(jnp.bfloat16)
    values = jnp.dot(sequence, w_value, preferred_element_type=jnp.float32).astype(jnp.bfloat16)
    queries = queries.astype(jnp.float32).reshape(length, KV_HEADS, group, HEAD_DIM)
    keys = keys.astype(jnp.float32).reshape(length, KV_HEADS, HEAD_DIM)
    values = values.astype(jnp.float32).reshape(length, KV_HEADS, HEAD_DIM)
    scores = jnp.einsum('qkgd,skd->kgqs', queries, keys) * (1.0 / math.sqrt(HEAD_DIM))
    causal = jnp.arange(length)[:, None] >= jnp.arange(length)[None, :]
    scores = jnp.where(causal, scores, -jnp.inf)
    top = lax.optimization_barrier(jnp.max(scores, axis=-1, keepdims=True))
    weights = jnp.exp(scores - top)
    probs = (weights / lax.optimization_barrier(jnp.sum(weights, axis=-1, keepdims=True))).astype(jnp.bfloat16)
    mixed = jnp.einsum('kgqs,skd->qkgd', probs.astype(jnp.float32), values)
    return mixed.reshape(length, HEADS * HEAD_DIM).astype(jnp.bfloat16)

def expert_block(block_rows, expert, w_gate, w_up, w_down):
    slices = N_DP * N_SECTION
    width = FFW // slices
    gate_rows = lax.dynamic_index_in_dim(w_gate, expert, 0, keepdims=False)
    up_rows = lax.dynamic_index_in_dim(w_up, expert, 0, keepdims=False)
    down_rows = lax.dynamic_index_in_dim(w_down, expert, 0, keepdims=False)
    contract = (((1,), (1,)), ((), ()))
    gate = lax.dot_general(block_rows, gate_rows, contract, preferred_element_type=jnp.float32)
    lifted = lax.dot_general(block_rows, up_rows, contract, preferred_element_type=jnp.float32)
    active = (jax.nn.silu(gate) * lifted).astype(jnp.bfloat16)
    active = active.astype(jnp.float32).reshape(BLOCK, slices, width)
    down = down_rows.astype(jnp.float32).reshape(slices, width, D)
    partial_value = jnp.einsum('tsh,shd->std', active, down)
    partial_value = lax.optimization_barrier(partial_value.astype(jnp.bfloat16)).astype(jnp.float32)
    return lax.optimization_barrier(jnp.sum(partial_value, axis=0)).astype(jnp.bfloat16)

def reference(tokens, w_query, w_key, w_value, w_out, w_gate, w_up, w_down, route, old_out, cotangent):
    replicas = N_DP * N_SECTION
    sequences = tokens.reshape(replicas, SEQ, D)
    routes = route.reshape(replicas, NB)
    olds = old_out.reshape(replicas, NB, BLOCK, D)
    cotangents = cotangent.reshape(replicas, SEQ, D)

    def one_replica(total, item):
        sequence, seq_routes, seq_old, seq_cot = item
        heads_out = attend_all(sequence, w_query, w_key, w_value)
        attention = jnp.dot(heads_out, w_out, preferred_element_type=jnp.float32)
        hidden_in = (sequence.astype(jnp.float32) + attention).astype(jnp.bfloat16)
        blocks_in = hidden_in.reshape(NB, BLOCK, D)
        expert_out = lax.map(lambda pair: expert_block(pair[0], pair[1], w_gate, w_up, w_down), (blocks_in, seq_routes))
        joined = (blocks_in.astype(jnp.float32) + expert_out.astype(jnp.float32)).astype(jnp.bfloat16)
        gap = joined.astype(jnp.float32) - seq_old.astype(jnp.float32)
        fresh = (seq_routes >= OLD).astype(jnp.float32)
        divergence = 0.5 * lax.optimization_barrier(jnp.mean(gap * gap, axis=-1)) * fresh[:, None]
        term = jnp.dot(seq_cot.T, heads_out, preferred_element_type=jnp.float32)
        term = lax.optimization_barrier(term.astype(jnp.bfloat16)).astype(jnp.float32)
        return (total + term, (joined, divergence))
    start = jnp.zeros((D, HEADS * HEAD_DIM), jnp.float32)
    grad, (joined, divergence) = lax.scan(one_replica, start, (sequences, routes, olds, cotangents))
    return (joined.reshape(NBT, BLOCK, D), divergence.reshape(NBT, BLOCK), grad)
```

```python
import math

import jax
import jax.numpy as jnp
from jax import lax
from jax.sharding import Mesh
from jax.sharding import PartitionSpec as P

HEAD_DIM = 128
BLOCK = 64
GROUP = ("outer", "section")


def attend_local(tokens, w_query, w_key, w_value):
    length = tokens.shape[0]
    key_heads = w_key.shape[1] // HEAD_DIM
    group = w_query.shape[1] // w_key.shape[1]
    queries = jnp.dot(tokens, w_query, preferred_element_type=jnp.float32).astype(jnp.bfloat16)
    queries = queries.reshape(length, key_heads, group, HEAD_DIM)
    keys = jnp.dot(tokens, w_key, preferred_element_type=jnp.float32).astype(jnp.bfloat16)
    keys = keys.reshape(length, key_heads, HEAD_DIM)
    values = jnp.dot(tokens, w_value, preferred_element_type=jnp.float32).astype(jnp.bfloat16)
    values = values.reshape(length, key_heads, HEAD_DIM)
    scores = jnp.einsum("qkgd,skd->kgqs", queries, keys, preferred_element_type=jnp.float32)
    scores = scores * (1.0 / math.sqrt(HEAD_DIM))
    query_pos = lax.broadcasted_iota(jnp.int32, (length, length), 0)
    key_pos = lax.broadcasted_iota(jnp.int32, (length, length), 1)
    scores = jnp.where(query_pos >= key_pos, scores, -jnp.inf)
    top = jnp.max(scores, axis=-1, keepdims=True)
    weights = jnp.exp(scores - top)
    probs = (weights / jnp.sum(weights, axis=-1, keepdims=True)).astype(jnp.bfloat16)
    mixed = jnp.einsum("kgqs,skd->qkgd", probs, values, preferred_element_type=jnp.float32)
    return mixed.astype(jnp.bfloat16).reshape(length, key_heads * group * HEAD_DIM)


def routing_table(routes, experts, capacity):
    number = routes.shape[0]
    same = routes[:, None] == routes[None, :]
    earlier = lax.broadcasted_iota(jnp.int32, (number, number), 1) < lax.broadcasted_iota(
        jnp.int32, (number, number), 0
    )
    slot = jnp.sum((same & earlier).astype(jnp.int32), axis=1)
    expert_hit = routes[None, :] == lax.broadcasted_iota(jnp.int32, (experts, number), 0)
    slot_hit = slot[None, :] == lax.broadcasted_iota(jnp.int32, (capacity, number), 0)
    return (expert_hit[:, None, :] & slot_hit[None, :, :]).astype(jnp.bfloat16)


def swap(value, axis):
    return lax.ppermute(value, axis, [(0, 1), (1, 0)])


def both(value, axis=0):
    if lax.axis_size("pair") == 1:
        return value
    return jnp.concatenate([value, swap(value, "pair")], axis=axis)


def pick(blocks, table):
    rows = jnp.einsum("cb,brd->crd", table, blocks, preferred_element_type=jnp.float32)
    return rows.astype(jnp.bfloat16)


def wo_gradient(cotangent, heads_out):
    length, width = cotangent.shape
    outer, pair = lax.axis_size("outer"), lax.axis_size("pair")
    parts = cotangent.reshape(length, outer, pair, width // (outer * pair))
    mine = lax.axis_index("pair")

    def part(number):
        return lax.dynamic_index_in_dim(parts, number, 2, keepdims=False).reshape(length, width // pair)

    left = part(mine)
    if pair == 2:
        left = jnp.concatenate([left, swap(part(1 - mine), "pair")], axis=0)
    term = lax.dot_general(
        left, both(heads_out), (((0,), (0,)), ((), ())), preferred_element_type=jnp.float32
    ).astype(jnp.bfloat16)
    return lax.psum_scatter(term, GROUP, scatter_dimension=0, tiled=True).astype(jnp.float32)


def per_device(
    tokens, w_query, w_key, w_value, w_out, w_gate, w_up, w_down, route, old_out, cotangent
):
    experts = lax.axis_size("expert")
    own = lax.axis_index("expert")
    length, width = tokens.shape
    blocks = length // BLOCK
    piece_rows = BLOCK // experts
    capacity = max(2, blocks // experts + 1)
    old_count = experts - max(1, experts // 4)
    routes = route[:, 0]
    table = routing_table(routes, experts, capacity)
    own_table = lax.dynamic_index_in_dim(table, own, 0, keepdims=False)
    token_rows = pick(tokens.reshape(blocks, BLOCK, width), own_table)

    heads_out = attend_local(tokens, w_query, w_key, w_value)
    head_blocks = heads_out.reshape(blocks, BLOCK, heads_out.shape[1])

    def project(rows):
        return jnp.dot(
            rows.reshape(-1, rows.shape[-1]), w_out, preferred_element_type=jnp.float32
        ).reshape(rows.shape[:-1] + (width,))

    if experts == 2:
        half = capacity * BLOCK // 2
        peer_table = lax.dynamic_index_in_dim(table, 1 - own, 0, keepdims=False)
        outgoing = project(pick(head_blocks, peer_table)).astype(jnp.bfloat16).reshape(-1, width)
        kept = project(pick(head_blocks, own_table)).reshape(-1, width)
        kept = kept + token_rows.reshape(-1, width).astype(jnp.float32)
        first = (kept[:half] + swap(outgoing[:half], "expert").astype(jnp.float32)).astype(jnp.bfloat16)
        second = (kept[half:] + swap(outgoing[half:], "expert").astype(jnp.float32)).astype(jnp.bfloat16)
    else:
        half = capacity * BLOCK // 2
        rows = jnp.einsum("jcb,brd->jcrd", table, head_blocks, preferred_element_type=jnp.float32)
        outgoing = project(rows.astype(jnp.bfloat16)).astype(jnp.bfloat16)
        total = lax.psum_scatter(outgoing, "expert", scatter_dimension=0, tiled=True)[0]
        total = (token_rows.astype(jnp.float32) + total.astype(jnp.float32)).astype(jnp.bfloat16)
        total = total.reshape(-1, width)
        first, second = total[:half], total[half:]

    gradient = wo_gradient(cotangent, heads_out)
    gate_rows, up_rows, down_rows = both(w_gate[0]), both(w_up[0]), both(w_down[0])
    contract = (((1,), (1,)), ((), ()))

    def expert(top, bottom):
        rows = jnp.concatenate([top, bottom], axis=0)
        gate = lax.dot_general(rows, gate_rows, contract, preferred_element_type=jnp.float32)
        lifted = lax.dot_general(rows, up_rows, contract, preferred_element_type=jnp.float32)
        active = (jax.nn.silu(gate) * lifted).astype(jnp.bfloat16)
        return jnp.dot(active, down_rows, preferred_element_type=jnp.float32)

    outer, section = lax.axis_size("outer"), lax.axis_size("section")
    ring = []
    for line in range(outer):
        places = [line * section + place for place in range(section)]
        ring += places if line % 2 == 0 else places[::-1]
    count = len(ring)
    onward = [(ring[i], ring[(i + 1) % count]) for i in range(count)]
    backward = [(target, source) for source, target in onward]
    front, back = first, second
    sums = None
    for _ in range(count - 1):
        front = lax.ppermute(front, GROUP, onward)
        back = lax.ppermute(back, GROUP, backward)
        terms = expert(front, back)
        upper, lower = terms[:half], terms[half:]
        if sums is not None:
            upper = upper + lax.ppermute(sums[0], GROUP, onward).astype(jnp.float32)
            lower = lower + lax.ppermute(sums[1], GROUP, backward).astype(jnp.float32)
        sums = (upper.astype(jnp.bfloat16), lower.astype(jnp.bfloat16))
    terms = expert(first, second)
    upper = terms[:half] + lax.ppermute(sums[0], GROUP, onward).astype(jnp.float32)
    lower = terms[half:] + lax.ppermute(sums[1], GROUP, backward).astype(jnp.float32)
    expert_sum = jnp.concatenate([upper, lower], axis=0)
    hidden = jnp.concatenate([first, second], axis=0).astype(jnp.float32)
    whole = (hidden + expert_sum.astype(jnp.bfloat16).astype(jnp.float32)).astype(jnp.bfloat16)
    whole = whole.reshape(capacity, experts, piece_rows, width)
    if experts == 2:
        mine = lax.dynamic_index_in_dim(whole, own, 1, keepdims=False)
        theirs = swap(lax.dynamic_index_in_dim(whole, 1 - own, 1, keepdims=False), "expert")
        joined = jnp.einsum("cb,crd->brd", own_table, mine, preferred_element_type=jnp.float32)
        joined = joined + jnp.einsum("cb,crd->brd", peer_table, theirs, preferred_element_type=jnp.float32)
    else:
        returned = lax.all_to_all(
            whole.transpose(1, 0, 2, 3), "expert", split_axis=0, concat_axis=0, tiled=True
        )
        joined = jnp.einsum("jcb,jcrd->brd", table, returned, preferred_element_type=jnp.float32)
    joined = joined.astype(jnp.bfloat16)
    fresh = (routes >= old_count).astype(jnp.float32)
    gap = joined.astype(jnp.float32) - old_out.astype(jnp.float32)
    divergence = 0.5 * jnp.mean(gap * gap, axis=-1) * fresh[:, None]
    return (joined, divergence, gradient)


def solution(mesh):
    sizes = mesh.shape
    pair = 2 if sizes["dp"] % 2 == 0 else 1
    split = Mesh(
        mesh.devices.reshape(sizes["dp"] // pair, pair, sizes["section"], sizes["expert"]),
        ("outer", "pair", "section", "expert"),
    )
    replicas = ("outer", "pair", "section")
    return jax.shard_map(
        per_device,
        mesh=split,
        in_specs=(
            P(replicas, None),
            P(None, "expert"),
            P(None, "expert"),
            P(None, "expert"),
            P("expert", None),
            P("expert", replicas, None),
            P("expert", replicas, None),
            P("expert", replicas, None),
            P(replicas, None),
            P(replicas, "expert", None),
            P(replicas, None),
        ),
        out_specs=(
            P(replicas, "expert", None),
            P(replicas, "expert"),
            P(replicas, "expert"),
        ),
        check_vma=False,
    )
```
